128 devices in a mesh: row: 4 (over x_hi, core), sector: 32 (over x_lo, y, z).
Axes of the slice: x: 4 (x_hi: 2, x_lo: 2; x = x_hi * 2 + x_lo), y: 4, z: 4, core: 2. Of those that a mesh axis runs over, the one named last changes fastest.
Arguments:
- state: float32 [6, 256, 512, 128], P(None, 'row', 'sector'), may hold values from -6 to 6
- interp_blocks: float32 [16, 16, 32], replicated, may hold values from -0.1 to 0.8
- rotor_offset: int32 [4, 3], replicated, may hold values from 0 to 511
- axial_speed: float32 [6], replicated, may hold values from 0.3 to 1.5
- row_swirl: float32 [4], P('row'), may hold values from -1.5 to 1.5
- diffusivity: float32 [6], replicated, may hold values from 0.05 to 0.3
- coupling: float32 [6, 6], replicated, may hold values from -1.5 to 1.5
Outputs:
- advanced: float32 [6, 256, 512, 128], P(None, 'row', 'sector')
The draws below stay inside these ranges and needn't reach their ends.
All inputs are finite; a program needn't handle non-finite values.
Results may differ from the reference program's by a relative error of at most 0.0001.
Values sent between devices are 32-bit elements; how exact they have to be, the bound alone decides.
A program may use at most 128 MiB of HBM per device.

```python
import math
import jax
import jax.numpy as jnp
from jax import lax

FIELDS = 6
SECTIONS = 4
CA = 64
CT = 16
CR = 128
ROWS = 4
INTERFACES = 3
NA = 256
NT = 512
N_ROW = 4
N_SECTOR = 32


def draw_interp_blocks(key, part):
    cell_ids = jnp.arange(CT)[:, None, None]
    target_ids = jnp.arange(CT)[None, :, None]
    source_ids = jnp.arange(2 * CT)[None, None, :]
    main_weight = jnp.where(source_ids == target_ids + cell_ids, 0.7, 0.0)
    side_weight = jnp.where(source_ids == target_ids + cell_ids + 1, 0.3, 0.0)
    spread = 0.15 / jnp.sqrt(2.0 * CT)
    noise = jax.random.truncated_normal(jax.random.fold_in(key, 11), -3.0, 3.0, (CT, CT, 2 * CT), jnp.float32)
    values = main_weight + side_weight + spread * noise
    return jnp.clip(values, -0.1, 0.8).astype(jnp.float32)


def touch_ends(values, stream_key, least, high):
    shape = values.shape
    spot = [jax.random.randint(jax.random.fold_in(stream_key, axis), (), 0, shape[axis]) for axis in range(len(shape))]
    values = values.at[tuple(spot)].set(least)
    longest = shape.index(max(shape))
    spot[longest] = (spot[longest] + 1) % shape[longest]
    return values.at[tuple(spot)].set(high)


def steps_of(stream_key, shape, cuts, smallest, largest):
    def one(axis_at, parts):
        heights = jax.random.uniform(jax.random.fold_in(jax.random.fold_in(stream_key, 6), axis_at), (parts,), jnp.float32, smallest / len(cuts), largest / len(cuts))
        return jnp.repeat(jnp.exp(heights), shape[axis_at] // parts).reshape((-1,) + (1,) * (len(shape) - axis_at - 1))

    loudness = one(*cuts[0])
    for cut in cuts[1:]:
        loudness = loudness * one(*cut)
    return loudness


def gaussian(rng, shape, scale, most, split=(), held_as=jnp.bfloat16):
    values = scale * jax.random.normal(rng, shape, jnp.float32)
    if split:
        values = values * steps_of(rng, shape, split, -0.22, 0.18)
    return jnp.clip(values, -most, most).astype(held_as)


def setup_inputs(seed: int = 0) -> dict:
    key_of = jax.random.split(jax.random.key(seed), 8)
    state = gaussian(key_of[0], (FIELDS, NA, NT, CR), 1.0, 6.0, ((1, 4), (2, 32)), jnp.float32)
    interp_blocks = draw_interp_blocks(jax.random.fold_in(key_of[7], 71), 0)
    rotor_offset = touch_ends(jax.random.randint(key_of[2], (SECTIONS, INTERFACES), 0, NT), jax.random.fold_in(key_of[2], 1), 0, NT - 1).astype(jnp.int32)
    axial_speed = jnp.clip(jnp.exp(jax.random.uniform(key_of[3], (FIELDS,), jnp.float32, math.log(0.3), math.log(1.5))), 0.3, 1.5)
    row_swirl = jnp.clip(jax.random.uniform(key_of[4], (ROWS,), jnp.float32, -1.5, 1.5) * steps_of(key_of[4], (ROWS,), ((0, 4),), -0.4, 0.0), -1.5, 1.5)
    diffusivity = jnp.clip(jnp.exp(jax.random.uniform(key_of[5], (FIELDS,), jnp.float32, math.log(0.05), math.log(0.3))), 0.05, 0.3)
    coupling = gaussian(key_of[6], (FIELDS, FIELDS), 0.3, 1.5, (), jnp.float32)
    return dict(state=state, interp_blocks=interp_blocks, rotor_offset=rotor_offset, axial_speed=axial_speed, row_swirl=row_swirl, diffusivity=diffusivity, coupling=coupling)


time_step = 0.4
highest = lax.Precision.HIGHEST


def residual_of(center, axial_pad, cycle_pad, axial_speed, swirl_speed, diffusivity, coupling):
    d_axial = (-axial_pad[:, 4:] + 8.0 * axial_pad[:, 3:-1] - 8.0 * axial_pad[:, 1:-3] + axial_pad[:, :-4]) / 12.0
    l_axial = (-axial_pad[:, 4:] + 16.0 * axial_pad[:, 3:-1] - 30.0 * center + 16.0 * axial_pad[:, 1:-3] - axial_pad[:, :-4]) / 12.0
    d_cycle = (-cycle_pad[:, :, 4:] + 8.0 * cycle_pad[:, :, 3:-1] - 8.0 * cycle_pad[:, :, 1:-3] + cycle_pad[:, :, :-4]) / 12.0
    l_cycle = (-cycle_pad[:, :, 4:] + 16.0 * cycle_pad[:, :, 3:-1] - 30.0 * center + 16.0 * cycle_pad[:, :, 1:-3] - cycle_pad[:, :, :-4]) / 12.0
    radial_pad = jnp.pad(center, ((0, 0), (0, 0), (0, 0), (1, 1)))
    l_radial = radial_pad[..., 2:] - 2.0 * center + radial_pad[..., :-2]
    mixing = jnp.einsum("fg,gatr->fatr", coupling, center, precision=highest)
    speed_col = axial_speed[:, None, None, None]
    diff_col = diffusivity[:, None, None, None]
    return -speed_col * d_axial - swirl_speed * d_cycle + diff_col * (l_axial + l_cycle + l_radial) + mixing


def interface(planes, offset, interp_blocks):
    sector_shift = offset // CT
    cell_shift = offset % CT
    blocks = planes.reshape(FIELDS, 2, N_SECTOR, CT, CR)
    first_part = jnp.roll(blocks, -sector_shift, axis=2)
    second_part = jnp.roll(first_part, -1, axis=2)
    paired = jnp.concatenate([first_part, second_part], axis=3)
    weights = interp_blocks[cell_shift]
    result = jnp.einsum("jk,faskr->fasjr", weights, paired, precision=highest)
    return result.reshape(FIELDS, 2, NT, CR)


def reference(state, interp_blocks, rotor_offset, axial_speed, row_swirl, diffusivity, coupling):
    def residual(current, section_index):
        blade_rows = current.reshape(FIELDS, N_ROW, CA, NT, CR)
        pieces = []
        for row_number in range(N_ROW):
            center = blade_rows[:, row_number]
            empty = jnp.zeros_like(center[:, :2])
            if row_number > 0:
                ghost_up = interface(blade_rows[:, row_number - 1, CA - 2:], rotor_offset[section_index, row_number - 1], interp_blocks)
            else:
                ghost_up = empty
            if row_number < N_ROW - 1:
                ghost_down = interface(blade_rows[:, row_number + 1, :2], (NT - rotor_offset[section_index, row_number]) % NT, interp_blocks)
            else:
                ghost_down = empty
            axial_pad = jnp.concatenate([ghost_up, center, ghost_down], axis=1)
            cycle_pad = jnp.concatenate([center[:, :, NT - 2:], center, center[:, :, :2]], axis=2)
            pieces.append(residual_of(center, axial_pad, cycle_pad, axial_speed, row_swirl[row_number], diffusivity, coupling))
        return jnp.concatenate(pieces, axis=1)

    first_rate = residual(state, 0)
    second_rate = residual(state + (0.5 * time_step) * first_rate, 1)
    third_rate = residual(state + (0.5 * time_step) * second_rate, 2)
    fourth_rate = residual(state + time_step * third_rate, 3)
    return state + (time_step / 6.0) * (first_rate + 2.0 * second_rate + 2.0 * third_rate + fourth_rate)
```

```python
import functools

import jax
import jax.numpy as jnp
from jax import lax
from jax.experimental import pallas as pl
from jax.experimental.pallas import tpu as pltpu
from jax.sharding import PartitionSpec as P

MESH = pl.DeviceIdType.MESH
H = 0.4
F = 6
CA = 64
CT = 16
CR = 128
G = 4
LO = 8
GROUPS = ((2, 22), (22, 42), (42, 62))
CHUNKS = GROUPS + ((0, 2), (62, 64))
PIECE = (F, 2, CT, CR)


def kernel(
    state, weights, offset, speed, swirl, diffusivity, coupling, out, q, *rest
):
    held = [[rest[(g * 2 + s) * 5 : (g * 2 + s) * 5 + 5] for s in range(2)] for g in range(G)]
    load_sem, halo_send, halo_recv, one_send, one_recv, two_send, two_recv, three_send, three_recv = rest[40:]
    row = lax.axis_index("row")
    sector = lax.axis_index("sector")
    x = sector // 16
    y = (sector // 4) % 4
    z = sector % 4
    after = (sector + 1) % 32
    before = (sector + 31) % 32
    flipped = (sector + 16) % 32

    def active(side):
        return row >= 1 if side == 0 else row <= 2

    def sends(side):
        return row <= 2 if side == 0 else row >= 1

    def load(i):
        a, b = CHUNKS[i]
        return pltpu.make_async_copy(
            state.at[:, a:b], q.at[0, :, a + 2 : b + 2, LO : LO + CT, :], load_sem.at[i]
        )

    def halo(g, i, up):
        a, b = CHUNKS[i]
        source, target = (LO + CT - 2, LO - 2) if up else (LO, LO + CT)
        return pltpu.make_async_remote_copy(
            src_ref=q.at[g, :, a + 2 : b + 2, source : source + 2, :],
            dst_ref=q.at[g, :, a + 2 : b + 2, target : target + 2, :],
            send_sem=halo_send.at[g, i, up],
            recv_sem=halo_recv.at[g, i, up],
            device_id=(row, after if up else before),
            device_id_type=MESH,
        )

    def one(g, side, flip, slot):
        a = CA if side == 0 else 2
        return pltpu.make_async_remote_copy(
            src_ref=q.at[g, :, a : a + 2, LO : LO + CT, :],
            dst_ref=held[g][side][0].at[slot],
            send_sem=one_send.at[g, side, flip],
            recv_sem=one_recv.at[g, side, slot],
            device_id=(row + 1 if side == 0 else row - 1, flipped if flip else sector),
            device_id_type=MESH,
        )

    def two(g, side, d):
        return pltpu.make_async_remote_copy(
            src_ref=held[g][side][1].at[d - 1],
            dst_ref=held[g][side][2].at[y],
            send_sem=two_send.at[g, side, d - 1],
            recv_sem=two_recv.at[g, side, d - 1],
            device_id=(row, x * 16 + ((y + d) % 4) * 4 + z),
            device_id_type=MESH,
        )

    def three(g, side, d):
        return pltpu.make_async_remote_copy(
            src_ref=held[g][side][3].at[d - 1],
            dst_ref=held[g][side][4].at[z],
            send_sem=three_send.at[g, side, d - 1],
            recv_sem=three_recv.at[g, side, d - 1],
            device_id=(row, x * 16 + y * 4 + (z + d) % 4),
            device_id_type=MESH,
        )

    def digits(g, side):
        if side == 0:
            o = offset[g, jnp.maximum(row - 1, 0)]
        else:
            o = (512 - offset[g, jnp.minimum(row, 2)]) & 511
        return (o >> 8) & 1, (o >> 6) & 3, (o >> 4) & 3, o & 15

    def send_one(g):
        for side in range(2):

            @pl.when(sends(side))
            def _():
                for flip in range(2):
                    one(g, side, flip, x).start()

    def send_two(g):
        for side in range(2):

            @pl.when(active(side))
            def _():
                for slot in range(2):
                    one(g, side, 0, slot).wait_recv()
                sx, sy, sz, _ = digits(g, side)
                first, staged, second, _, _ = held[g][side]
                for d in range(4):
                    target = (y + d) % 4
                    role = jnp.where(((target + sy) & 3) == y, 0, 1)
                    pick = (x + sx + ((target + sy + role) >> 2)) & 1
                    content = first[pick]
                    if d == 0:
                        second[y] = content
                    else:
                        staged[d - 1] = content
                        two(g, side, d).start()

    def send_three(g):
        for side in range(2):

            @pl.when(active(side))
            def _():
                for d in range(1, 4):
                    two(g, side, d).wait_recv()
                sx, sy, sz, _ = digits(g, side)
                _, _, second, staged, third = held[g][side]
                for d in range(4):
                    target = (z + d) % 4
                    role = jnp.where(((target + sz) & 3) == z, 0, 1)
                    pick = (y + sy + ((target + sz + role) >> 2)) & 3
                    content = second[pick]
                    if d == 0:
                        third[z] = content
                    else:
                        staged[d - 1] = content
                        three(g, side, d).start()

    def ghosts(g):
        for side in range(2):
            a = 0 if side == 0 else CA + 2

            @pl.when(active(side))
            def _():
                for d in range(1, 4):
                    three(g, side, d).wait_recv()
                _, _, sz, cell = digits(g, side)
                third = held[g][side][4]
                near = third[(z + sz) & 3]
                far = third[(z + sz + 1) & 3]
                w = weights[cell]
                block = jnp.concatenate(
                    [
                        jnp.concatenate([near[f, p], far[f, p]], axis=0)
                        for f in range(F)
                        for p in range(2)
                    ],
                    axis=1,
                )
                got = jnp.dot(
                    w, block, precision=lax.Precision.HIGHEST, preferred_element_type=jnp.float32
                )
                for f in range(F):
                    for p in range(2):
                        n = (f * 2 + p) * CR
                        q[g, f, a + p, LO : LO + CT, :] = got[:, n : n + CR]

            @pl.when(jnp.logical_not(active(side)))
            def _():
                for f in range(F):
                    for p in range(2):
                        q[g, f, a + p, LO : LO + CT, :] = jnp.zeros((CT, CR), jnp.float32)

    lane = lax.broadcasted_iota(jnp.int32, (8, CR), 1)

    def splat(value):
        return jnp.full((8, CR), value, jnp.float32)

    def advance(g, planes):
        scale = (H / 2, H / 2, H, H / 6)[g]

        def field(f, _):
            d = splat(diffusivity[f]) * scale
            s = splat(speed[f]) * scale
            w = splat(swirl[0]) * scale
            mix = [splat(coupling[f, e]) * scale for e in range(F)]
            near_d, far_d = d * (16.0 / 12.0), d * (-1.0 / 12.0)
            a_p1, a_m1 = near_d - s * (8.0 / 12.0), near_d + s * (8.0 / 12.0)
            a_p2, a_m2 = far_d + s * (1.0 / 12.0), far_d - s * (1.0 / 12.0)
            c_p1, c_m1 = near_d - w * (8.0 / 12.0), near_d + w * (8.0 / 12.0)
            c_p2, c_m2 = far_d + w * (1.0 / 12.0), far_d - w * (1.0 / 12.0)
            centre = d * -7.0
            from_left = jnp.where(lane == 0, 0.0, d)
            from_right = jnp.where(lane == CR - 1, 0.0, d)

            def plane(a):
                for half in range(2):
                    t = LO + 8 * half

                    def at(field, by_a, by_t):
                        return q[g, field, a + 2 + by_a, t + by_t : t + by_t + 8, :]

                    own = at(f, 0, 0)
                    total = centre * own
                    for e in range(F):
                        total += mix[e] * at(e, 0, 0)
                    total += from_left * pltpu.roll(own, 1, 1)
                    total += from_right * pltpu.roll(own, CR - 1, 1)
                    ring = c_p1 * at(f, 0, 1) + c_m1 * at(f, 0, -1)
                    ring += c_p2 * at(f, 0, 2) + c_m2 * at(f, 0, -2)
                    along = a_p1 * at(f, 1, 0) + a_m1 * at(f, -1, 0)
                    along += a_p2 * at(f, 2, 0) + a_m2 * at(f, -2, 0)
                    total += ring + along

                    def stage(n):
                        return q[n, f, a + 2, t : t + 8, :]

                    if g < G - 1:
                        q[g + 1, f, a + 2, t : t + 8, :] = stage(0) + total
                    else:
                        out[f, a, 8 * half : 8 * half + 8, :] = total + (
                            stage(1) + 2.0 * stage(2) + own - stage(0)
                        ) * (1.0 / 3.0)

            if isinstance(planes[0], tuple):
                for a, b in planes:
                    for n in range(a, b):
                        plane(n)
            else:

                def pair(n, _):
                    plane(planes[0] + 2 * n)
                    plane(planes[0] + 2 * n + 1)
                    return 0

                lax.fori_loop(0, (planes[1] - planes[0]) // 2, pair, 0)
            return 0

        lax.fori_loop(0, F, field, 0)

    for i in (3, 4, 0, 1, 2):
        load(i).start()
    barrier = pltpu.get_barrier_semaphore()

    def greet(r, s):
        pl.semaphore_signal(barrier, inc=1, device_id=(r, s), device_id_type=MESH)

    greet(row, after)
    greet(row, before)
    for d in range(1, 4):
        greet(row, x * 16 + ((y + d) % 4) * 4 + z)
        greet(row, x * 16 + y * 4 + (z + d) % 4)

    @pl.when(row <= 2)
    def _():
        greet(row + 1, sector)
        greet(row + 1, flipped)

    @pl.when(row >= 1)
    def _():
        greet(row - 1, sector)
        greet(row - 1, flipped)

    pl.semaphore_wait(barrier, jnp.where(row == 0, 10, jnp.where(row == 3, 10, 12)))

    load(3).wait()
    load(4).wait()
    send_one(0)
    for i in (0, 3, 4, 1, 2):
        if i < 3:
            load(i).wait()
        for up in range(2):
            halo(0, i, up).start()

    for g in range(G):

        def group(i):
            for up in range(2):
                halo(g, i, up).wait_recv()
            advance(g, CHUNKS[i])
            if g < G - 1:
                for up in range(2):
                    halo(g + 1, i, up).start()

        group(0)
        send_two(g)
        group(1)
        send_three(g)
        group(2)
        ghosts(g)
        for i in (3, 4):
            for up in range(2):
                halo(g, i, up).wait_recv()
        advance(g, (CHUNKS[3], CHUNKS[4]))
        if g < G - 1:
            send_one(g + 1)
            for i in (3, 4):
                for up in range(2):
                    halo(g + 1, i, up).start()

    for g in range(G):
        for i in range(5):
            for up in range(2):
                halo(g, i, up).wait_send()
        for side in range(2):

            @pl.when(sends(side))
            def _():
                for flip in range(2):
                    one(g, side, flip, x).wait_send()

            @pl.when(active(side))
            def _():
                for d in range(1, 4):
                    two(g, side, d).wait_send()
                    three(g, side, d).wait_send()


def on_device(state, interp_blocks, rotor_offset, axial_speed, row_swirl, diffusivity, coupling):
    smem = pl.BlockSpec(memory_space=pltpu.SMEM)
    vmem = pl.BlockSpec(memory_space=pltpu.VMEM)
    held = []
    for _ in range(2 * G):
        for n in (2, 3, 4, 3, 4):
            held.append(pltpu.VMEM((n,) + PIECE, jnp.float32))
    dma = pltpu.SemaphoreType.DMA
    return pl.pallas_call(
        kernel,
        out_shape=jax.ShapeDtypeStruct(state.shape, jnp.float32),
        in_specs=[pl.BlockSpec(memory_space=pl.ANY), vmem, smem, smem, smem, smem, smem],
        out_specs=vmem,
        scratch_shapes=[
            pltpu.VMEM((G, F, CA + 4, 32, CR), jnp.float32),
            *held,
            dma((5,)),
            dma((G, 5, 2)),
            dma((G, 5, 2)),
            dma((G, 2, 2)),
            dma((G, 2, 2)),
            dma((G, 2, 3)),
            dma((G, 2, 3)),
            dma((G, 2, 3)),
            dma((G, 2, 3)),
        ],
        compiler_params=pltpu.CompilerParams(
            collective_id=0, has_side_effects=True, vmem_limit_bytes=64 * 1024 * 1024 - 65536
        ),
    )(state, interp_blocks, rotor_offset, axial_speed, row_swirl, diffusivity, coupling)


def solution(mesh):
    return jax.shard_map(
        on_device,
        mesh=mesh,
        in_specs=(P(None, "row", "sector", None), P(), P(), P(), P("row"), P(), P()),
        out_specs=P(None, "row", "sector", None),
        check_vma=False,
    )
```

```python
import functools

import jax
import jax.numpy as jnp
from jax import lax
from jax.experimental import pallas as pl
from jax.experimental.pallas import tpu as pltpu
from jax.sharding import PartitionSpec as P

MESH = pl.DeviceIdType.MESH
H = 0.4
F = 6
CA = 64
CT = 16
CR = 128
G = 4
LO = 8
STEP = 4
UNITS = tuple((2 + 12 * i, 14 + 12 * i, 3 * j, 3 * j + 3) for i in range(5) for j in range(2))
CHUNKS = UNITS + ((0, 2, 0, 6), (62, 64, 0, 6))
LOADS = ((0, 2), (62, 64)) + tuple((2 + 12 * i, 14 + 12 * i) for i in range(5))
N = len(UNITS)
ORDER = "CC2HC2HC2HC3HCHC3HCH3CHC4H4H4"
PIECES = 3
PF = F // PIECES
PIECE = (PF, 2, CT, CR)


def kernel(
    state, small_0, small_1, small_2, small_3, small_4, small_5, out, result, q0, q1, q2, q3, *rest
):
    q = (q0, q1, q2, q3)
    weights, offset, speed, swirl, diffusivity, coupling = rest[:6]
    rest = rest[6:]
    held = [
        [[rest[((g * 2 + s) * PIECES + p) * 5 :][:5] for p in range(PIECES)] for s in range(2)]
        for g in range(G)
    ]
    small = (
        (small_0, weights),
        (small_1, offset),
        (small_2, speed),
        (small_3, swirl),
        (small_4, diffusivity),
        (small_5, coupling),
    )
    small_sem, load_sem, store_sem, halo_send, halo_recv, turn_send, turn_recv = rest[
        2 * G * PIECES * 5 :
    ]
    row = lax.axis_index("row")
    sector = lax.axis_index("sector")
    x = sector // 16
    y = (sector // 4) % 4
    z = sector % 4
    after = (sector + 1) % 32
    before = (sector + 31) % 32
    flipped = (sector + 16) % 32

    def active(side):
        return row >= 1 if side == 0 else row <= 2

    def sends(side):
        return row <= 2 if side == 0 else row >= 1

    def load(i):
        a, b = LOADS[i]
        return pltpu.make_async_copy(
            state.at[:, a:b], q[0].at[:, a + 2 : b + 2, LO : LO + CT, :], load_sem.at[i]
        )

    def arrived(like, sem):
        pltpu.make_async_copy(like, like, sem).wait()

    def wait_halo(g, i):
        a, b, f, e = CHUNKS[i]
        arrived(q[g].at[f:e, a + 2 : b + 2, 0:4, :], halo_recv.at[g, i])

    def store(i):
        a, b, f, e = CHUNKS[i]
        return pltpu.make_async_copy(
            result.at[f:e, a:b], out.at[f:e, a:b], store_sem
        )

    def halo(g, i, up):
        a, b, f, e = CHUNKS[i]
        source, target = (LO + CT - 2, LO - 2) if up else (LO, LO + CT)
        return pltpu.make_async_remote_copy(
            src_ref=q[g].at[f:e, a + 2 : b + 2, source : source + 2, :],
            dst_ref=q[g].at[f:e, a + 2 : b + 2, target : target + 2, :],
            send_sem=halo_send.at[g],
            recv_sem=halo_recv.at[g, i],
            device_id=(row, after if up else before),
            device_id_type=MESH,
        )

    def one(g, side, p, flip, slot):
        a = CA if side == 0 else 2
        return pltpu.make_async_remote_copy(
            src_ref=q[g].at[PF * p : PF * p + PF, a : a + 2, LO : LO + CT, :],
            dst_ref=held[g][side][p][0].at[slot],
            send_sem=turn_send.at[0, side],
            recv_sem=turn_recv.at[0, g, side, p],
            device_id=(row + 1 if side == 0 else row - 1, flipped if flip else sector),
            device_id_type=MESH,
        )

    def two(g, side, p, d):
        return pltpu.make_async_remote_copy(
            src_ref=held[g][side][p][1].at[d - 1],
            dst_ref=held[g][side][p][2].at[y],
            send_sem=turn_send.at[1, side],
            recv_sem=turn_recv.at[1, g, side, p],
            device_id=(row, x * 16 + ((y + d) % 4) * 4 + z),
            device_id_type=MESH,
        )

    def three(g, side, p, d):
        return pltpu.make_async_remote_copy(
            src_ref=held[g][side][p][3].at[d - 1],
            dst_ref=held[g][side][p][4].at[z],
            send_sem=turn_send.at[2, side],
            recv_sem=turn_recv.at[2, g, side, p],
            device_id=(row, x * 16 + y * 4 + (z + d) % 4),
            device_id_type=MESH,
        )

    def digits(g, side):
        if side == 0:
            o = offset[g, jnp.maximum(row - 1, 0)]
        else:
            o = (512 - offset[g, jnp.minimum(row, 2)]) & 511
        return (o >> 8) & 1, (o >> 6) & 3, (o >> 4) & 3, o & 15

    def send_one(g, p):
        for side in range(2):

            @pl.when(sends(side))
            def _():
                for flip in range(2):
                    one(g, side, p, flip, x).start()

    def send_two(g, p):
        for side in range(2):

            @pl.when(active(side))
            def _():
                arrived(held[g][side][p][0], turn_recv.at[0, g, side, p])
                sx, sy, sz, _ = digits(g, side)
                first, staged, second, _, _ = held[g][side][p]
                for d in (1, 3, 2, 0):
                    target = (y + d) % 4
                    role = jnp.where(((target + sy) & 3) == y, 0, 1)
                    pick = (x + sx + ((target + sy + role) >> 2)) & 1
                    content = first[pick]
                    if d == 0:
                        second[y] = content
                    else:
                        staged[d - 1] = content
                        two(g, side, p, d).start()

    def send_three(g, p):
        for side in range(2):

            @pl.when(active(side))
            def _():
                arrived(held[g][side][p][1], turn_recv.at[1, g, side, p])
                sx, sy, sz, _ = digits(g, side)
                _, _, second, staged, third = held[g][side][p]
                for d in (1, 3, 2, 0):
                    target = (z + d) % 4
                    role = jnp.where(((target + sz) & 3) == z, 0, 1)
                    pick = (y + sy + ((target + sz + role) >> 2)) & 3
                    content = second[pick]
                    if d == 0:
                        third[z] = content
                    else:
                        staged[d - 1] = content
                        three(g, side, p, d).start()

    def clear():
        for side in range(2):
            a = 0 if side == 0 else CA + 2

            @pl.when(jnp.logical_not(active(side)))
            def _():
                for g in range(G):
                    q[g][:, a : a + 2, LO : LO + CT, :] = jnp.zeros((F, 2, CT, CR), jnp.float32)

    def ghosts(g, p):
        for side in range(2):
            a = 0 if side == 0 else CA + 2

            @pl.when(active(side))
            def _():
                arrived(held[g][side][p][3], turn_recv.at[2, g, side, p])
                _, _, sz, cell = digits(g, side)
                third = held[g][side][p][4]
                near = third[(z + sz) & 3]
                far = third[(z + sz + 1) & 3]
                w = weights[cell]
                block = jnp.concatenate(
                    [
                        jnp.concatenate([near[f, n], far[f, n]], axis=0)
                        for f in range(PF)
                        for n in range(2)
                    ],
                    axis=1,
                )
                got = jnp.dot(
                    w, block, precision=lax.Precision.HIGHEST, preferred_element_type=jnp.float32
                )
                for f in range(PF):
                    for n in range(2):
                        at = (f * 2 + n) * CR
                        q[g][PF * p + f, a + n, LO : LO + CT, :] = got[:, at : at + CR]

    lane = lax.broadcasted_iota(jnp.int32, (8, CR), 1)

    def splat(value):
        return jnp.full((8, CR), value, jnp.float32)

    def coefficients(g, f):
        scale = (H / 2, H / 2, H, H / 6)[g]
        d = splat(diffusivity[f]) * scale
        s = splat(speed[f]) * scale
        w = splat(swirl[0]) * scale
        mix = [
            splat(coupling[f, e]) * scale + jnp.where(splat_int(f) == e, d * -7.0, 0.0)
            for e in range(F)
        ]
        near_d, far_d = d * (16.0 / 12.0), d * (-1.0 / 12.0)
        near_s, far_s = s * (8.0 / 12.0), s * (1.0 / 12.0)
        near_w, far_w = w * (8.0 / 12.0), w * (1.0 / 12.0)
        along = (far_d - far_s, near_d + near_s, near_d - near_s, far_d + far_s)
        ring = (far_d - far_w, near_d + near_w, near_d - near_w, far_d + far_w)
        left = jnp.where(lane == 0, 0.0, d)
        right = jnp.where(lane == CR - 1, 0.0, d)
        return mix, along, ring, left, right

    def splat_int(value):
        return jnp.full((8, CR), value, jnp.int32)

    def block(g, f, coefs, a, n):
        mix, along, ring, left, right = coefs
        now = q[g]
        results = []
        for half in range(2):
            t = LO + 8 * half
            window = [now[f, a + i, t : t + 8, :] for i in range(n + 4)]
            for i in range(n):
                own = window[i + 2]
                plane = a + i + 2
                parts = [mix[e] * now[e, plane, t : t + 8, :] for e in range(F)]
                parts += [along[j] * window[i + (0, 1, 3, 4)[j]] for j in range(4)]
                parts += [
                    ring[j] * now[f, plane, t + (-2, -1, 1, 2)[j] : t + (6, 7, 9, 10)[j], :]
                    for j in range(4)
                ]
                parts += [left * pltpu.roll(own, 1, 1), right * pltpu.roll(own, CR - 1, 1)]
                if g == 0:
                    parts.append(own)
                elif g < G - 1:
                    parts.append(q[0][f, plane, t : t + 8, :])
                else:
                    two_q2 = q[2][f, plane, t : t + 8, :] * 2.0
                    three_s = q[1][f, plane, t : t + 8, :] - q[0][f, plane, t : t + 8, :]
                    parts.append(((two_q2 + three_s) + own) * (1.0 / 3.0))
                sums = [parts[0] + parts[6], parts[1] + parts[7], parts[2] + parts[8]]
                sums += [parts[3] + parts[9], parts[4] + parts[10], parts[5] + parts[11]]
                sums += [parts[12] + parts[14], parts[13] + parts[15] + parts[16]]
                total = ((sums[0] + sums[1]) + (sums[2] + sums[3])) + (
                    (sums[4] + sums[5]) + (sums[6] + sums[7])
                )
                results.append((plane, t, total))
        for plane, t, total in results:
            if g < G - 1:
                q[g + 1][f, plane, t : t + 8, :] = total
            else:
                result[f, plane - 2, t - LO : t - LO + 8, :] = total

    def interior(g, i):
        start, stop, low, high = CHUNKS[i]

        def field(f, _):
            coefs = coefficients(g, f)

            def step(n, _):
                block(g, f, coefs, start + STEP * n, STEP)
                return 0

            lax.fori_loop(0, (stop - start) // STEP, step, 0)
            return 0

        lax.fori_loop(low, high, field, 0)

    def edges(g, p):
        def field(i, _):
            f = PF * p + i
            coefs = coefficients(g, f)
            block(g, f, coefs, 0, 2)
            block(g, f, coefs, CA - 2, 2)
            return 0

        lax.fori_loop(0, PF, field, 0)

    def fetch(i):
        return pltpu.make_async_copy(small[i][0], small[i][1], small_sem.at[i])

    for i in range(6):
        fetch(i).start()
    for i in range(len(LOADS)):
        load(i).start()
    barrier = pltpu.get_barrier_semaphore()

    def greet(r, s):
        pl.semaphore_signal(barrier, inc=1, device_id=(r, s), device_id_type=MESH)

    greet(row, after)
    greet(row, before)
    for d in range(1, 4):
        greet(row, x * 16 + ((y + d) % 4) * 4 + z)
        greet(row, x * 16 + y * 4 + (z + d) % 4)

    @pl.when(row <= 2)
    def _():
        greet(row + 1, sector)
        greet(row + 1, flipped)

    @pl.when(row >= 1)
    def _():
        greet(row - 1, sector)
        greet(row - 1, flipped)

    for i in range(6):
        fetch(i).wait()
    clear()
    pl.semaphore_wait(barrier, jnp.where(row == 0, 10, jnp.where(row == 3, 10, 12)))

    load(0).wait()
    load(1).wait()
    for p in range(PIECES):
        send_one(0, p)

    def send_halo(g, i):
        for up in range(2):
            halo(g, i, up).start()

    for n in range(5):
        load(2 + n).wait()
        if n < 2:
            send_halo(0, 2 * n)
            send_halo(0, 2 * n + 1)
    send_halo(0, N)
    send_halo(0, N + 1)

    for g in range(G):
        last = g == G - 1
        done, sent, steps = 0, 0, {"2": 0, "3": 0, "4": 0}
        for what in ORDER:
            if what == "C":
                wait_halo(g, done)
                interior(g, done)
                if last:
                    store(done).start()
                if g == 0 and done + 4 < N:
                    send_halo(0, done + 4)
                done += 1
            elif what == "H":
                if not last:
                    send_halo(g + 1, sent)
                sent += 1
            else:
                p = steps[what]
                steps[what] += 1
                if what == "2":
                    send_two(g, p)
                elif what == "3":
                    send_three(g, p)
                else:
                    if p == 0:
                        for i in (N, N + 1):
                            wait_halo(g, i)
                    ghosts(g, p)
                    edges(g, p)
                    if not last:
                        send_one(g + 1, p)
        for i in (N, N + 1):
            if last:
                store(i).start()
            else:
                send_halo(g + 1, i)

    arrived(result, store_sem)
    for g in range(G):
        arrived(q[g].at[:, 2 : CA + 2, 0:4, :], halo_send.at[g])
    for side in range(2):

        @pl.when(sends(side))
        def _():
            arrived(q[0].at[:, 0 : 2 * G, :, :], turn_send.at[0, side])

        @pl.when(active(side))
        def _():
            for n in range(1, 3):
                arrived(q[0].at[:, 0 : 3 * G, :, :], turn_send.at[n, side])


def on_device(state, interp_blocks, rotor_offset, axial_speed, row_swirl, diffusivity, coupling):
    def keep(value):
        return pltpu.with_memory_space_constraint(value, pltpu.HBM)

    interp_blocks, rotor_offset, coupling = keep(interp_blocks), keep(rotor_offset), keep(coupling)
    axial_speed, diffusivity = keep(axial_speed), keep(diffusivity)
    hbm = pl.BlockSpec(memory_space=pltpu.HBM)
    held = []
    for _ in range(2 * G * PIECES):
        for n in (2, 3, 4, 3, 4):
            held.append(pltpu.VMEM((n,) + PIECE, jnp.float32))
    dma = pltpu.SemaphoreType.DMA
    return pl.pallas_call(
        kernel,
        out_shape=jax.ShapeDtypeStruct(state.shape, jnp.float32),
        in_specs=[hbm] * 7,
        out_specs=pl.BlockSpec(memory_space=pl.ANY),
        scratch_shapes=[
            pltpu.VMEM(state.shape, jnp.float32),
            *[pltpu.VMEM((F, CA + 4, 32, CR), jnp.float32) for _ in range(G)],
            pltpu.VMEM(interp_blocks.shape, jnp.float32),
            pltpu.SMEM(rotor_offset.shape, jnp.int32),
            pltpu.SMEM(axial_speed.shape, jnp.float32),
            pltpu.SMEM(row_swirl.shape, jnp.float32),
            pltpu.SMEM(diffusivity.shape, jnp.float32),
            pltpu.SMEM(coupling.shape, jnp.float32),
            *held,
            dma((6,)),
            dma((len(LOADS),)),
            dma,
            dma((G,)),
            dma((G, N + 2)),
            dma((3, 2)),
            dma((3, G, 2, PIECES)),
        ],
        compiler_params=pltpu.CompilerParams(
            collective_id=0, has_side_effects=True, vmem_limit_bytes=48 * 1024 * 1024
        ),
    )(state, interp_blocks, rotor_offset, axial_speed, row_swirl, diffusivity, coupling)


def solution(mesh):
    return jax.shard_map(
        on_device,
        mesh=mesh,
        in_specs=(P(None, "row", "sector", None), P(), P(), P(), P("row"), P(), P()),
        out_specs=P(None, "row", "sector", None),
        check_vma=False,
    )
```

```python
import functools

import jax
import jax.numpy as jnp
from jax import lax
from jax.experimental import pallas as pl
from jax.experimental.pallas import tpu as pltpu
from jax.sharding import PartitionSpec as P

MESH = pl.DeviceIdType.MESH
H = 0.4
F = 6
CA = 64
CT = 16
CR = 128
G = 4
LO = 8
STEP = 12
UNITS = tuple((2 + 12 * i, 14 + 12 * i, 3 * j, 3 * j + 3) for i in range(5) for j in range(2))
CHUNKS = UNITS + ((0, 2, 0, 6), (62, 64, 0, 6))
LOADS = ((0, 2), (62, 64)) + tuple((2 + 12 * i, 14 + 12 * i) for i in range(5))
N = len(UNITS)
ORDER = "CHCHC2HC2HC2HC3HC3HC3HCC4H4H4"
PIECES = 3
PF = F // PIECES
PIECE = (PF, 2, CT, CR)


def kernel(
    state, small_0, small_1, small_2, small_3, small_4, small_5, out, result, q0, q1, q2, q3, *rest
):
    q = (q0, q1, q2, q3)
    weights, offset, speed, swirl, diffusivity, coupling = rest[:6]
    rest = rest[6:]
    held = [
        [[rest[((g * 2 + s) * PIECES + p) * 5 :][:5] for p in range(PIECES)] for s in range(2)]
        for g in range(G)
    ]
    small = (
        (small_0, weights),
        (small_1, offset),
        (small_2, speed),
        (small_3, swirl),
        (small_4, diffusivity),
        (small_5, coupling),
    )
    small_sem, load_sem, store_sem, halo_send, halo_recv, turn_send, turn_recv = rest[
        2 * G * PIECES * 5 :
    ]
    row = lax.axis_index("row")
    sector = lax.axis_index("sector")
    x = sector // 16
    y = (sector // 4) % 4
    z = sector % 4
    after = (sector + 1) % 32
    before = (sector + 31) % 32
    flipped = (sector + 16) % 32

    def active(side):
        return row >= 1 if side == 0 else row <= 2

    def sends(side):
        return row <= 2 if side == 0 else row >= 1

    def load(i):
        a, b = LOADS[i]
        return pltpu.make_async_copy(
            state.at[:, a:b], q[0].at[:, a + 2 : b + 2, LO : LO + CT, :], load_sem.at[i]
        )

    def arrived(like, sem):
        pltpu.make_async_copy(like, like, sem).wait()

    def wait_halo(g, i):
        a, b, f, e = CHUNKS[i]
        arrived(q[g].at[f:e, a + 2 : b + 2, 0:4, :], halo_recv.at[g, i])

    def store(i):
        a, b, f, e = CHUNKS[i]
        return pltpu.make_async_copy(
            result.at[f:e, a:b], out.at[f:e, a:b], store_sem
        )

    def halo(g, i, up):
        a, b, f, e = CHUNKS[i]
        source, target = (LO + CT - 2, LO - 2) if up else (LO, LO + CT)
        return pltpu.make_async_remote_copy(
            src_ref=q[g].at[f:e, a + 2 : b + 2, source : source + 2, :],
            dst_ref=q[g].at[f:e, a + 2 : b + 2, target : target + 2, :],
            send_sem=halo_send.at[g],
            recv_sem=halo_recv.at[g, i],
            device_id=(row, after if up else before),
            device_id_type=MESH,
        )

    def one(g, side, p, flip, slot):
        a = CA if side == 0 else 2
        return pltpu.make_async_remote_copy(
            src_ref=q[g].at[PF * p : PF * p + PF, a : a + 2, LO : LO + CT, :],
            dst_ref=held[g][side][p][0].at[slot],
            send_sem=turn_send.at[0, side],
            recv_sem=turn_recv.at[0, g, side, p],
            device_id=(row + 1 if side == 0 else row - 1, flipped if flip else sector),
            device_id_type=MESH,
        )

    def two(g, side, p, d):
        return pltpu.make_async_remote_copy(
            src_ref=held[g][side][p][1].at[d - 1],
            dst_ref=held[g][side][p][2].at[y],
            send_sem=turn_send.at[1, side],
            recv_sem=turn_recv.at[1, g, side, p],
            device_id=(row, x * 16 + ((y + d) % 4) * 4 + z),
            device_id_type=MESH,
        )

    def three(g, side, p, d):
        return pltpu.make_async_remote_copy(
            src_ref=held[g][side][p][3].at[d - 1],
            dst_ref=held[g][side][p][4].at[z],
            send_sem=turn_send.at[2, side],
            recv_sem=turn_recv.at[2, g, side, p],
            device_id=(row, x * 16 + y * 4 + (z + d) % 4),
            device_id_type=MESH,
        )

    def digits(g, side):
        if side == 0:
            o = offset[g, jnp.maximum(row - 1, 0)]
        else:
            o = (512 - offset[g, jnp.minimum(row, 2)]) & 511
        return (o >> 8) & 1, (o >> 6) & 3, (o >> 4) & 3, o & 15

    def send_one(g, p):
        for side in range(2):

            @pl.when(sends(side))
            def _():
                for flip in range(2):
                    one(g, side, p, flip, x).start()

    def send_two(g, p):
        for side in range(2):

            @pl.when(active(side))
            def _():
                arrived(held[g][side][p][0], turn_recv.at[0, g, side, p])
                sx, sy, sz, _ = digits(g, side)
                first, staged, second, _, _ = held[g][side][p]
                for d in (1, 3, 2, 0):
                    target = (y + d) % 4
                    role = jnp.where(((target + sy) & 3) == y, 0, 1)
                    pick = (x + sx + ((target + sy + role) >> 2)) & 1
                    content = first[pick]
                    if d == 0:
                        second[y] = content
                    else:
                        staged[d - 1] = content
                        two(g, side, p, d).start()

    def send_three(g, p):
        for side in range(2):

            @pl.when(active(side))
            def _():
                arrived(held[g][side][p][1], turn_recv.at[1, g, side, p])
                sx, sy, sz, _ = digits(g, side)
                _, _, second, staged, third = held[g][side][p]
                for d in (1, 3, 2, 0):
                    target = (z + d) % 4
                    role = jnp.where(((target + sz) & 3) == z, 0, 1)
                    pick = (y + sy + ((target + sz + role) >> 2)) & 3
                    content = second[pick]
                    if d == 0:
                        third[z] = content
                    else:
                        staged[d - 1] = content
                        three(g, side, p, d).start()

    def clear():
        for side in range(2):
            a = 0 if side == 0 else CA + 2

            @pl.when(jnp.logical_not(active(side)))
            def _():
                for g in range(G):
                    q[g][:, a : a + 2, LO : LO + CT, :] = jnp.zeros((F, 2, CT, CR), jnp.float32)

    def ghosts(g, p):
        for side in range(2):
            a = 0 if side == 0 else CA + 2

            @pl.when(active(side))
            def _():
                arrived(held[g][side][p][3], turn_recv.at[2, g, side, p])
                _, _, sz, cell = digits(g, side)
                third = held[g][side][p][4]
                near = third[(z + sz) & 3]
                far = third[(z + sz + 1) & 3]
                w = weights[cell]
                block = jnp.concatenate(
                    [
                        jnp.concatenate([near[f, n], far[f, n]], axis=0)
                        for f in range(PF)
                        for n in range(2)
                    ],
                    axis=1,
                )
                got = jnp.dot(
                    w, block, precision=lax.Precision.HIGHEST, preferred_element_type=jnp.float32
                )
                for f in range(PF):
                    for n in range(2):
                        at = (f * 2 + n) * CR
                        q[g][PF * p + f, a + n, LO : LO + CT, :] = got[:, at : at + CR]

    lane = lax.broadcasted_iota(jnp.int32, (8, CR), 1)

    def splat(value):
        return jnp.full((8, CR), value, jnp.float32)

    def coefficients(g, f):
        scale = (H / 2, H / 2, H, H / 6)[g]
        d = splat(diffusivity[f]) * scale
        s = splat(speed[f]) * scale
        w = splat(swirl[0]) * scale
        mix = [
            splat(coupling[f, e]) * scale + jnp.where(splat_int(f) == e, d * -7.0, 0.0)
            for e in range(F)
        ]
        near_d, far_d = d * (16.0 / 12.0), d * (-1.0 / 12.0)
        near_s, far_s = s * (8.0 / 12.0), s * (1.0 / 12.0)
        near_w, far_w = w * (8.0 / 12.0), w * (1.0 / 12.0)
        along = (far_d - far_s, near_d + near_s, near_d - near_s, far_d + far_s)
        ring = (far_d - far_w, near_d + near_w, near_d - near_w, far_d + far_w)
        left = jnp.where(lane == 0, 0.0, d)
        right = jnp.where(lane == CR - 1, 0.0, d)
        return mix, along, ring, left, right

    def splat_int(value):
        return jnp.full((8, CR), value, jnp.int32)

    def block(g, f, coefs, a, n):
        mix, along, ring, left, right = coefs
        now = q[g]
        results = []
        for half in range(2):
            t = LO + 8 * half
            window = [now[f, a + i, t : t + 8, :] for i in range(n + 4)]
            for i in range(n):
                own = window[i + 2]
                plane = a + i + 2
                parts = [mix[e] * now[e, plane, t : t + 8, :] for e in range(F)]
                parts += [along[j] * window[i + (0, 1, 3, 4)[j]] for j in range(4)]
                parts += [
                    ring[j] * now[f, plane, t + (-2, -1, 1, 2)[j] : t + (6, 7, 9, 10)[j], :]
                    for j in range(4)
                ]
                parts += [left * pltpu.roll(own, 1, 1), right * pltpu.roll(own, CR - 1, 1)]
                if g == 0:
                    parts.append(own)
                elif g < G - 1:
                    parts.append(q[0][f, plane, t : t + 8, :])
                else:
                    two_q2 = q[2][f, plane, t : t + 8, :] * 2.0
                    three_s = q[1][f, plane, t : t + 8, :] - q[0][f, plane, t : t + 8, :]
                    parts.append(((two_q2 + three_s) + own) * (1.0 / 3.0))
                sums = [parts[0] + parts[6], parts[1] + parts[7], parts[2] + parts[8]]
                sums += [parts[3] + parts[9], parts[4] + parts[10], parts[5] + parts[11]]
                sums += [parts[12] + parts[14], parts[13] + parts[15] + parts[16]]
                total = ((sums[0] + sums[1]) + (sums[2] + sums[3])) + (
                    (sums[4] + sums[5]) + (sums[6] + sums[7])
                )
                results.append((plane, t, total))
        for plane, t, total in results:
            if g < G - 1:
                q[g + 1][f, plane, t : t + 8, :] = total
            else:
                result[f, plane - 2, t - LO : t - LO + 8, :] = total

    def interior(g, i):
        start, stop, low, high = CHUNKS[i]

        def field(f, _):
            coefs = coefficients(g, f)

            def step(n, _):
                block(g, f, coefs, start + STEP * n, STEP)
                return 0

            lax.fori_loop(0, (stop - start) // STEP, step, 0)
            return 0

        lax.fori_loop(low, high, field, 0)

    def edges(g, p):
        def field(i, _):
            f = PF * p + i
            coefs = coefficients(g, f)
            block(g, f, coefs, 0, 2)
            block(g, f, coefs, CA - 2, 2)
            return 0

        lax.fori_loop(0, PF, field, 0)

    def fetch(i):
        return pltpu.make_async_copy(small[i][0], small[i][1], small_sem.at[i])

    for i in range(6):
        fetch(i).start()
    for i in range(len(LOADS)):
        load(i).start()
    barrier = pltpu.get_barrier_semaphore()

    def greet(r, s):
        pl.semaphore_signal(barrier, inc=1, device_id=(r, s), device_id_type=MESH)

    greet(row, after)
    greet(row, before)
    for d in range(1, 4):
        greet(row, x * 16 + ((y + d) % 4) * 4 + z)
        greet(row, x * 16 + y * 4 + (z + d) % 4)

    @pl.when(row <= 2)
    def _():
        greet(row + 1, sector)
        greet(row + 1, flipped)

    @pl.when(row >= 1)
    def _():
        greet(row - 1, sector)
        greet(row - 1, flipped)

    for i in range(6):
        fetch(i).wait()
    clear()
    pl.semaphore_wait(barrier, jnp.where(row == 0, 10, jnp.where(row == 3, 10, 12)))

    load(0).wait()
    load(1).wait()
    for p in range(PIECES):
        send_one(0, p)

    def send_halo(g, i):
        for up in range(2):
            halo(g, i, up).start()

    for n in range(5):
        load(2 + n).wait()
        for i in (2 * n, 2 * n + 1):
            if i < N - ORDER.count("P"):
                send_halo(0, i)
    send_halo(0, N)
    send_halo(0, N + 1)

    for g in range(G):
        last = g == G - 1
        left = N - ORDER.count("P")
        done, sent, steps = 0, 0, {"2": 0, "3": 0, "4": 0}
        for what in ORDER:
            if what == "C":
                wait_halo(g, done)
                interior(g, done)
                if last:
                    store(done).start()
                done += 1
            elif what == "P":
                send_halo(g, left)
                left += 1
            elif what == "H":
                if not last:
                    send_halo(g + 1, sent)
                sent += 1
            else:
                p = steps[what]
                steps[what] += 1
                if what == "2":
                    send_two(g, p)
                elif what == "3":
                    send_three(g, p)
                else:
                    if p == 0:
                        for i in (N, N + 1):
                            wait_halo(g, i)
                    ghosts(g, p)
                    edges(g, p)
                    if not last:
                        send_one(g + 1, p)
        for i in (N, N + 1):
            if last:
                store(i).start()
            else:
                send_halo(g + 1, i)

    arrived(result, store_sem)
    for g in range(G):
        arrived(q[g].at[:, 2 : CA + 2, 0:4, :], halo_send.at[g])
    for side in range(2):

        @pl.when(sends(side))
        def _():
            arrived(q[0].at[:, 0 : 2 * G, :, :], turn_send.at[0, side])

        @pl.when(active(side))
        def _():
            for n in range(1, 3):
                arrived(q[0].at[:, 0 : 3 * G, :, :], turn_send.at[n, side])


def on_device(state, interp_blocks, rotor_offset, axial_speed, row_swirl, diffusivity, coupling):
    def keep(value):
        return pltpu.with_memory_space_constraint(value, pltpu.HBM)

    interp_blocks, rotor_offset, coupling = keep(interp_blocks), keep(rotor_offset), keep(coupling)
    axial_speed, diffusivity = keep(axial_speed), keep(diffusivity)
    hbm = pl.BlockSpec(memory_space=pltpu.HBM)
    held = []
    for _ in range(2 * G * PIECES):
        for n in (2, 3, 4, 3, 4):
            held.append(pltpu.VMEM((n,) + PIECE, jnp.float32))
    dma = pltpu.SemaphoreType.DMA
    return pl.pallas_call(
        kernel,
        out_shape=jax.ShapeDtypeStruct(state.shape, jnp.float32),
        in_specs=[hbm] * 7,
        out_specs=pl.BlockSpec(memory_space=pl.ANY),
        scratch_shapes=[
            pltpu.VMEM(state.shape, jnp.float32),
            *[pltpu.VMEM((F, CA + 4, 32, CR), jnp.float32) for _ in range(G)],
            pltpu.VMEM(interp_blocks.shape, jnp.float32),
            pltpu.SMEM(rotor_offset.shape, jnp.int32),
            pltpu.SMEM(axial_speed.shape, jnp.float32),
            pltpu.SMEM(row_swirl.shape, jnp.float32),
            pltpu.SMEM(diffusivity.shape, jnp.float32),
            pltpu.SMEM(coupling.shape, jnp.float32),
            *held,
            dma((6,)),
            dma((len(LOADS),)),
            dma,
            dma((G,)),
            dma((G, N + 2)),
            dma((3, 2)),
            dma((3, G, 2, PIECES)),
        ],
        compiler_params=pltpu.CompilerParams(
            collective_id=0, has_side_effects=True, vmem_limit_bytes=48 * 1024 * 1024
        ),
    )(state, interp_blocks, rotor_offset, axial_speed, row_swirl, diffusivity, coupling)


def solution(mesh):
    return jax.shard_map(
        on_device,
        mesh=mesh,
        in_specs=(P(None, "row", "sector", None), P(), P(), P(), P("row"), P(), P()),
        out_specs=P(None, "row", "sector", None),
        check_vma=False,
    )
```

```python
import functools

import jax
import jax.numpy as jnp
from jax import lax
from jax.experimental import pallas as pl
from jax.experimental.pallas import tpu as pltpu
from jax.sharding import PartitionSpec as P

MESH = pl.DeviceIdType.MESH
H = 0.4
F = 6
CA = 64
CT = 16
CR = 128
G = 4
LO = 8
STEP = 12
UNITS = tuple((2 + 12 * i, 14 + 12 * i, 3 * j, 3 * j + 3) for i in range(5) for j in range(2))
CHUNKS = UNITS + ((0, 2, 0, 6), (62, 64, 0, 6))
LOADS = ((0, 2), (62, 64)) + tuple((2 + 12 * i, 14 + 12 * i) for i in range(5))
N = len(UNITS)
ORDER = "CHCHC2HC2HC2HC3HC3HC3HCC4H4H4"
PIECES = 3
PF = F // PIECES
PIECE = (PF, 2, CT, CR)


def kernel(
    state, small_0, small_1, small_2, small_3, small_4, small_5, out, result, q0, q1, q2, q3, *rest
):
    q = (q0, q1, q2, q3)
    weights, offset, speed, swirl, diffusivity, coupling = rest[:6]
    rest = rest[6:]
    held = [
        [[rest[((g * 2 + s) * PIECES + p) * 5 :][:5] for p in range(PIECES)] for s in range(2)]
        for g in range(G)
    ]
    small = (
        (small_0, weights),
        (small_1, offset),
        (small_2, speed),
        (small_3, swirl),
        (small_4, diffusivity),
        (small_5, coupling),
    )
    small_sem, load_sem, store_sem, halo_send, halo_recv, turn_send, turn_recv = rest[
        2 * G * PIECES * 5 :
    ]
    row = lax.axis_index("row")
    sector = lax.axis_index("sector")
    x = sector // 16
    y = (sector // 4) % 4
    z = sector % 4
    after = (sector + 1) % 32
    before = (sector + 31) % 32
    flipped = (sector + 16) % 32

    def active(side):
        return row >= 1 if side == 0 else row <= 2

    def sends(side):
        return row <= 2 if side == 0 else row >= 1

    def load(i):
        a, b = LOADS[i]
        return pltpu.make_async_copy(
            state.at[:, a:b], q[0].at[:, a + 2 : b + 2, LO : LO + CT, :], load_sem.at[i]
        )

    def arrived(like, sem):
        pltpu.make_async_copy(like, like, sem).wait()

    def wait_halo(g, i):
        a, b, f, e = CHUNKS[i]
        arrived(q[g].at[f:e, a + 2 : b + 2, 0:4, :], halo_recv.at[g, i])

    def store(i):
        a, b, f, e = CHUNKS[i]
        return pltpu.make_async_copy(
            result.at[f:e, a:b], out.at[f:e, a:b], store_sem
        )

    def store_edges(p):
        for a in (0, CA - 2):
            pltpu.make_async_copy(
                result.at[PF * p : PF * p + PF, a : a + 2],
                out.at[PF * p : PF * p + PF, a : a + 2],
                store_sem,
            ).start()

    def halo(g, i, up):
        a, b, f, e = CHUNKS[i]
        source, target = (LO + CT - 2, LO - 2) if up else (LO, LO + CT)
        return pltpu.make_async_remote_copy(
            src_ref=q[g].at[f:e, a + 2 : b + 2, source : source + 2, :],
            dst_ref=q[g].at[f:e, a + 2 : b + 2, target : target + 2, :],
            send_sem=halo_send.at[g],
            recv_sem=halo_recv.at[g, i],
            device_id=(row, after if up else before),
            device_id_type=MESH,
        )

    def one(g, side, p, flip, slot):
        a = CA if side == 0 else 2
        return pltpu.make_async_remote_copy(
            src_ref=q[g].at[PF * p : PF * p + PF, a : a + 2, LO : LO + CT, :],
            dst_ref=held[g][side][p][0].at[slot],
            send_sem=turn_send.at[0, side],
            recv_sem=turn_recv.at[0, g, side, p],
            device_id=(row + 1 if side == 0 else row - 1, flipped if flip else sector),
            device_id_type=MESH,
        )

    def two(g, side, p, d):
        return pltpu.make_async_remote_copy(
            src_ref=held[g][side][p][1].at[d - 1],
            dst_ref=held[g][side][p][2].at[y],
            send_sem=turn_send.at[1, side],
            recv_sem=turn_recv.at[1, g, side, p],
            device_id=(row, x * 16 + ((y + d) % 4) * 4 + z),
            device_id_type=MESH,
        )

    def three(g, side, p, d):
        return pltpu.make_async_remote_copy(
            src_ref=held[g][side][p][3].at[d - 1],
            dst_ref=held[g][side][p][4].at[z],
            send_sem=turn_send.at[2, side],
            recv_sem=turn_recv.at[2, g, side, p],
            device_id=(row, x * 16 + y * 4 + (z + d) % 4),
            device_id_type=MESH,
        )

    def digits(g, side):
        if side == 0:
            o = offset[g, jnp.maximum(row - 1, 0)]
        else:
            o = (512 - offset[g, jnp.minimum(row, 2)]) & 511
        return (o >> 8) & 1, (o >> 6) & 3, (o >> 4) & 3, o & 15

    def send_one(g, p):
        for side in range(2):

            @pl.when(sends(side))
            def _():
                for flip in range(2):
                    one(g, side, p, flip, x).start()

    def send_two(g, p):
        for side in range(2):

            @pl.when(active(side))
            def _():
                arrived(held[g][side][p][0], turn_recv.at[0, g, side, p])
                sx, sy, sz, _ = digits(g, side)
                first, staged, second, _, _ = held[g][side][p]
                for d in (2, 1, 3, 0):
                    target = (y + d) % 4
                    role = jnp.where(((target + sy) & 3) == y, 0, 1)
                    pick = (x + sx + ((target + sy + role) >> 2)) & 1
                    content = first[pick]
                    if d == 0:
                        second[y] = content
                    else:
                        staged[d - 1] = content
                        two(g, side, p, d).start()

    def send_three(g, p):
        for side in range(2):

            @pl.when(active(side))
            def _():
                arrived(held[g][side][p][1], turn_recv.at[1, g, side, p])
                sx, sy, sz, _ = digits(g, side)
                _, _, second, staged, third = held[g][side][p]
                for d in (2, 1, 3, 0):
                    target = (z + d) % 4
                    role = jnp.where(((target + sz) & 3) == z, 0, 1)
                    pick = (y + sy + ((target + sz + role) >> 2)) & 3
                    content = second[pick]
                    if d == 0:
                        third[z] = content
                    else:
                        staged[d - 1] = content
                        three(g, side, p, d).start()

    def clear():
        for side in range(2):
            a = 0 if side == 0 else CA + 2

            @pl.when(jnp.logical_not(active(side)))
            def _():
                for g in range(G):
                    q[g][:, a : a + 2, LO : LO + CT, :] = jnp.zeros((F, 2, CT, CR), jnp.float32)

    def ghosts(g, p):
        for side in range(2):
            a = 0 if side == 0 else CA + 2

            @pl.when(active(side))
            def _():
                arrived(held[g][side][p][3], turn_recv.at[2, g, side, p])
                _, _, sz, cell = digits(g, side)
                third = held[g][side][p][4]
                near = third[(z + sz) & 3]
                far = third[(z + sz + 1) & 3]
                w = weights[cell]
                block = jnp.concatenate(
                    [
                        jnp.concatenate([near[f, n], far[f, n]], axis=0)
                        for f in range(PF)
                        for n in range(2)
                    ],
                    axis=1,
                )
                got = jnp.dot(
                    w, block, precision=lax.Precision.HIGHEST, preferred_element_type=jnp.float32
                )
                for f in range(PF):
                    for n in range(2):
                        at = (f * 2 + n) * CR
                        q[g][PF * p + f, a + n, LO : LO + CT, :] = got[:, at : at + CR]

    lane = lax.broadcasted_iota(jnp.int32, (8, CR), 1)

    def splat(value):
        return jnp.full((8, CR), value, jnp.float32)

    def coefficients(g, f):
        scale = (H / 2, H / 2, H, H / 6)[g]
        d = splat(diffusivity[f]) * scale
        s = splat(speed[f]) * scale
        w = splat(swirl[0]) * scale
        mix = [
            splat(coupling[f, e]) * scale + jnp.where(splat_int(f) == e, d * -7.0, 0.0)
            for e in range(F)
        ]
        near_d, far_d = d * (16.0 / 12.0), d * (-1.0 / 12.0)
        near_s, far_s = s * (8.0 / 12.0), s * (1.0 / 12.0)
        near_w, far_w = w * (8.0 / 12.0), w * (1.0 / 12.0)
        along = (far_d - far_s, near_d + near_s, near_d - near_s, far_d + far_s)
        ring = (far_d - far_w, near_d + near_w, near_d - near_w, far_d + far_w)
        left = jnp.where(lane == 0, 0.0, d)
        right = jnp.where(lane == CR - 1, 0.0, d)
        return mix, along, ring, left, right

    def splat_int(value):
        return jnp.full((8, CR), value, jnp.int32)

    def block(g, f, coefs, a, n):
        mix, along, ring, left, right = coefs
        now = q[g]
        results = []
        for half in range(2):
            t = LO + 8 * half
            window = [now[f, a + i, t : t + 8, :] for i in range(n + 4)]
            for i in range(n):
                own = window[i + 2]
                plane = a + i + 2
                parts = [mix[e] * now[e, plane, t : t + 8, :] for e in range(F)]
                parts += [along[j] * window[i + (0, 1, 3, 4)[j]] for j in range(4)]
                parts += [
                    ring[j] * now[f, plane, t + (-2, -1, 1, 2)[j] : t + (6, 7, 9, 10)[j], :]
                    for j in range(4)
                ]
                parts += [left * pltpu.roll(own, 1, 1), right * pltpu.roll(own, CR - 1, 1)]
                if g == 0:
                    parts.append(own)
                elif g < G - 1:
                    parts.append(q[0][f, plane, t : t + 8, :])
                else:
                    two_q2 = q[2][f, plane, t : t + 8, :] * 2.0
                    three_s = q[1][f, plane, t : t + 8, :] - q[0][f, plane, t : t + 8, :]
                    parts.append(((two_q2 + three_s) + own) * (1.0 / 3.0))
                sums = [parts[0] + parts[6], parts[1] + parts[7], parts[2] + parts[8]]
                sums += [parts[3] + parts[9], parts[4] + parts[10], parts[5] + parts[11]]
                sums += [parts[12] + parts[14], parts[13] + parts[15] + parts[16]]
                total = ((sums[0] + sums[1]) + (sums[2] + sums[3])) + (
                    (sums[4] + sums[5]) + (sums[6] + sums[7])
                )
                results.append((plane, t, total))
        for plane, t, total in results:
            if g < G - 1:
                q[g + 1][f, plane, t : t + 8, :] = total
            else:
                result[f, plane - 2, t - LO : t - LO + 8, :] = total

    def interior(g, i):
        start, stop, low, high = CHUNKS[i]

        def field(f, _):
            coefs = coefficients(g, f)

            def step(n, _):
                block(g, f, coefs, start + STEP * n, STEP)
                return 0

            lax.fori_loop(0, (stop - start) // STEP, step, 0)
            return 0

        lax.fori_loop(low, high, field, 0)

    def edges(g, p):
        def field(i, _):
            f = PF * p + i
            coefs = coefficients(g, f)
            block(g, f, coefs, 0, 2)
            block(g, f, coefs, CA - 2, 2)
            return 0

        lax.fori_loop(0, PF, field, 0)

    def fetch(i):
        return pltpu.make_async_copy(small[i][0], small[i][1], small_sem.at[i])

    barrier = pltpu.get_barrier_semaphore()

    def greet(r, s):
        pl.semaphore_signal(barrier, inc=1, device_id=(r, s), device_id_type=MESH)

    greet(row, after)
    greet(row, before)
    for d in range(1, 4):
        greet(row, x * 16 + ((y + d) % 4) * 4 + z)
        greet(row, x * 16 + y * 4 + (z + d) % 4)

    @pl.when(row <= 2)
    def _():
        greet(row + 1, sector)
        greet(row + 1, flipped)

    @pl.when(row >= 1)
    def _():
        greet(row - 1, sector)
        greet(row - 1, flipped)

    for i in range(6):
        fetch(i).start()
    for i in range(len(LOADS)):
        load(i).start()
    for i in range(6):
        fetch(i).wait()
    clear()
    pl.semaphore_wait(barrier, jnp.where(row == 0, 10, jnp.where(row == 3, 10, 12)))

    load(0).wait()
    load(1).wait()
    for p in range(PIECES):
        send_one(0, p)

    def send_halo(g, i):
        for up in range(2):
            halo(g, i, up).start()

    for n in range(5):
        load(2 + n).wait()
        for i in (2 * n, 2 * n + 1):
            if i < N - ORDER.count("P"):
                send_halo(0, i)
    send_halo(0, N)
    send_halo(0, N + 1)

    for g in range(G):
        last = g == G - 1
        left = N - ORDER.count("P")
        done, sent, steps = 0, 0, {"2": 0, "3": 0, "4": 0}
        for what in ORDER:
            if what == "C":
                wait_halo(g, done)
                interior(g, done)
                if last:
                    store(done).start()
                done += 1
            elif what == "P":
                send_halo(g, left)
                left += 1
            elif what == "H":
                if not last:
                    send_halo(g + 1, sent)
                sent += 1
            else:
                p = steps[what]
                steps[what] += 1
                if what == "2":
                    send_two(g, p)
                elif what == "3":
                    send_three(g, p)
                else:
                    if p == 0:
                        for i in (N, N + 1):
                            wait_halo(g, i)
                    ghosts(g, p)
                    edges(g, p)
                    if last:
                        store_edges(p)
                    else:
                        send_one(g + 1, p)
        if not last:
            for i in (N, N + 1):
                send_halo(g + 1, i)

    arrived(result, store_sem)
    for g in range(G):
        arrived(q[g].at[:, 2 : CA + 2, 0:4, :], halo_send.at[g])
    for side in range(2):

        @pl.when(sends(side))
        def _():
            arrived(q[0].at[:, 0 : 2 * G, :, :], turn_send.at[0, side])

        @pl.when(active(side))
        def _():
            for n in range(1, 3):
                arrived(q[0].at[:, 0 : 3 * G, :, :], turn_send.at[n, side])


def on_device(state, interp_blocks, rotor_offset, axial_speed, row_swirl, diffusivity, coupling):
    def keep(value):
        return pltpu.with_memory_space_constraint(value, pltpu.HBM)

    interp_blocks, rotor_offset, coupling = keep(interp_blocks), keep(rotor_offset), keep(coupling)
    axial_speed, diffusivity = keep(axial_speed), keep(diffusivity)
    hbm = pl.BlockSpec(memory_space=pltpu.HBM)
    held = []
    for _ in range(2 * G * PIECES):
        for n in (2, 3, 4, 3, 4):
            held.append(pltpu.VMEM((n,) + PIECE, jnp.float32))
    dma = pltpu.SemaphoreType.DMA
    return pl.pallas_call(
        kernel,
        out_shape=jax.ShapeDtypeStruct(state.shape, jnp.float32),
        in_specs=[hbm] * 7,
        out_specs=pl.BlockSpec(memory_space=pl.ANY),
        scratch_shapes=[
            pltpu.VMEM(state.shape, jnp.float32),
            *[pltpu.VMEM((F, CA + 4, 32, CR), jnp.float32) for _ in range(G)],
            pltpu.VMEM(interp_blocks.shape, jnp.float32),
            pltpu.SMEM(rotor_offset.shape, jnp.int32),
            pltpu.SMEM(axial_speed.shape, jnp.float32),
            pltpu.SMEM(row_swirl.shape, jnp.float32),
            pltpu.SMEM(diffusivity.shape, jnp.float32),
            pltpu.SMEM(coupling.shape, jnp.float32),
            *held,
            dma((6,)),
            dma((len(LOADS),)),
            dma,
            dma((G,)),
            dma((G, N + 2)),
            dma((3, 2)),
            dma((3, G, 2, PIECES)),
        ],
        compiler_params=pltpu.CompilerParams(
            collective_id=0, has_side_effects=True, vmem_limit_bytes=48 * 1024 * 1024
        ),
    )(state, interp_blocks, rotor_offset, axial_speed, row_swirl, diffusivity, coupling)


def solution(mesh):
    return jax.shard_map(
        on_device,
        mesh=mesh,
        in_specs=(P(None, "row", "sector", None), P(), P(), P(), P("row"), P(), P()),
        out_specs=P(None, "row", "sector", None),
        check_vma=False,
    )
```
